32 devices in a mesh: group: 4 (over y, x), member: 8 (over z, core).
Axes of the slice: x: 2, y: 2, z: 4, core: 2. Of those that a mesh axis runs over, the one named last changes fastest.
Arguments:
- picture_embedding_matrix: bfloat16 [8192, 1152], P(('group', 'member')), may hold values from -1 to 1
- caption_embedding_matrix: bfloat16 [8192, 1152], P(('group', 'member')), may hold values from -1 to 1
- learned_sharpness: float32 [1], replicated, may hold values from 5 to 20
- learned_offset_entry: float32 [1], replicated, may hold values from -4 to -2
Outputs:
- grad_images: float32 [8192, 1152], P(('group', 'member'))
- grad_texts: float32 [8192, 1152], P(('group', 'member'))
The draws below stay inside these ranges and needn't reach their ends.
All inputs are finite; a program needn't handle non-finite values.
Results may differ from the reference program's by a relative error of at most 0.002.
Values may be sent and summed in bfloat16 or wider, within the bound.
A program may use at most 192 MiB of HBM per device.

```python
import math
import jax
import jax.numpy as jnp
from jax import lax

D = 1152
ROWS = 256
GROUP_ROWS = 2048
TOTAL = 8192
N_GROUP = 4
N_MEMBER = 8


def paired_rows(key):
    base_key = jax.random.fold_in(key, 7301)
    image_key, noise_key, ratio_key = jax.random.split(base_key, 3)
    spread = 1.0 / math.sqrt(D)
    picture_features = jnp.clip(spread * jax.random.normal(image_key, (TOTAL, D), jnp.float32), -5.0 * spread, 5.0 * spread)
    noise_rows = jnp.clip(spread * jax.random.normal(noise_key, (TOTAL, D), jnp.float32), -5.0 * spread, 5.0 * spread)
    pair_ratio = jax.random.uniform(ratio_key, (TOTAL, 1), jnp.float32, 0.15, 0.35)
    caption_features = pair_ratio * picture_features + jnp.sqrt(1.0 - pair_ratio * pair_ratio) * noise_rows
    caption_features = jnp.clip(caption_features, -1.0, 1.0)
    return (picture_features, caption_features)


def draw_picture_embedding_matrix(key, part):
    return paired_rows(key)[0].astype(jnp.bfloat16)


def draw_caption_embedding_matrix(key, part):
    return paired_rows(key)[1].astype(jnp.bfloat16)


def setup_inputs(seed: int = 0) -> dict:
    arg_keys = jax.random.split(jax.random.key(seed), 5)
    return {
        "picture_embedding_matrix": draw_picture_embedding_matrix(jax.random.fold_in(arg_keys[4], 71), 0),
        "caption_embedding_matrix": draw_caption_embedding_matrix(jax.random.fold_in(arg_keys[4], 71), 0),
        "learned_sharpness": jnp.clip(jnp.exp(jax.random.uniform(arg_keys[2], (1,), jnp.float32, math.log(5.0), math.log(20.0))), 5.0, 20.0),
        "learned_offset_entry": jnp.clip(jax.random.uniform(arg_keys[3], (1,), jnp.float32, -4.0, -2.0), -4.0, -2.0),
    }


def weighting_factors(similarity_scores, match_polarity, sharpness_multiplier):
    return (-sharpness_multiplier * match_polarity * jax.nn.sigmoid(-match_polarity * similarity_scores)).astype(jnp.bfloat16)


def reference(picture_embedding_matrix, caption_embedding_matrix, learned_sharpness, learned_offset_entry):
    sharpness_multiplier = learned_sharpness[0]
    offset_amount = learned_offset_entry[0]
    img_blocks = picture_embedding_matrix.reshape(N_GROUP, GROUP_ROWS, D)
    txt_blocks = caption_embedding_matrix.reshape(N_GROUP, GROUP_ROWS, D)
    txt_before = jnp.roll(txt_blocks, 1, axis=0)
    matching_polarity = jnp.eye(GROUP_ROWS, dtype=jnp.float32) * 2.0 - 1.0

    def one_group(block_groups):
        picture_features, caption_features, before = block_groups
        similarity_scores = sharpness_multiplier * jnp.dot(picture_features, caption_features.T, preferred_element_type=jnp.float32) + offset_amount
        score_multipliers = weighting_factors(similarity_scores, matching_polarity, sharpness_multiplier)
        grad_img = jnp.dot(score_multipliers, caption_features, preferred_element_type=jnp.float32)
        grad_txt = jnp.dot(score_multipliers.T, picture_features, preferred_element_type=jnp.float32)
        picture_participant = picture_features.reshape(N_MEMBER, ROWS, D).astype(jnp.float32)
        earlier_participant = before.reshape(N_MEMBER, ROWS, D).astype(jnp.float32)
        earlier_scores = sharpness_multiplier * jnp.einsum("eun,ean->eua", picture_participant, earlier_participant) + offset_amount
        earlier_multipliers = weighting_factors(earlier_scores, -1.0, sharpness_multiplier).astype(jnp.float32)
        grad_img = grad_img + jnp.einsum("mrs,msd->mrd", earlier_multipliers, earlier_participant).reshape(GROUP_ROWS, D)
        returned = jnp.einsum("mrs,mrd->msd", earlier_multipliers, picture_participant).reshape(GROUP_ROWS, D)
        return grad_img, grad_txt, returned

    grad_img, grad_txt, returned = lax.map(one_group, (img_blocks, txt_blocks, txt_before))
    grad_txt = grad_txt + jnp.roll(returned, -1, axis=0)
    return grad_img.reshape(TOTAL, D), grad_txt.reshape(TOTAL, D)
```

```python
import functools

import jax
import jax.numpy as jnp
from jax import lax
from jax.experimental import pallas as pl
from jax.experimental.pallas import tpu as pltpu
from jax.sharding import PartitionSpec as P

MESH = pl.DeviceIdType.MESH
F32 = jnp.float32
PIECES = 4


def contract(a, b, da, db):
    return lax.dot_general(a, b, (((da,), (db,)), ((), ())), preferred_element_type=F32)


def kernel(
    groups, n, sharp_ref, bias_ref, img_ref, txt_ref, gi_ref, gt_ref,
    other, gi_other, gi_in, txt_prev, img_next, tbuf, coef, gin, gout, vin, vout,
    t_send, t_recv, g_send, g_recv, v_send, v_recv, x_send, x_recv,
):
    rows, width = img_ref.shape
    piece = rows // PIECES
    group = lax.axis_index("group")
    member = lax.axis_index("member")
    chip, core = member // 2, member % 2
    partner = (group, member + 1 - 2 * core)
    ahead = ((group + 1) % groups, member)
    behind = ((group + groups - 1) % groups, member)
    right, left = (group, member + 2), (group, member - 2)
    has_right, has_left = chip + 1 < n, chip > 0
    sharp, bias = sharp_ref[0], bias_ref[0]

    barrier = pltpu.get_barrier_semaphore()
    for device in (partner, ahead, behind):
        pl.semaphore_signal(barrier, inc=1, device_id=device, device_id_type=MESH)
    for exists, device in ((has_right, right), (has_left, left)):
        @pl.when(exists)
        def _():
            pl.semaphore_signal(barrier, inc=1, device_id=device, device_id_type=MESH)
    pl.semaphore_wait(barrier, 3 + has_right.astype(jnp.int32) + has_left.astype(jnp.int32))

    def remote(src, dst, send, recv, device):
        return pltpu.make_async_remote_copy(
            src_ref=src, dst_ref=dst, send_sem=send, recv_sem=recv,
            device_id=device, device_id_type=MESH,
        )

    def own_text(slot, device):
        return remote(txt_ref, tbuf.at[chip], t_send.at[slot], t_recv.at[chip], device)

    def passed_text(b, device):
        return remote(tbuf.at[b], tbuf.at[b], t_send.at[b], t_recv.at[b], device)

    def sums(b, slot, p, device):
        return remote(gout.at[b, p], gin.at[slot, p], g_send.at[b, p], g_recv.at[slot, p], device)

    def means(b, slot, p, device):
        return remote(vout.at[b, p], vin.at[slot, p], v_send.at[b, p], v_recv.at[slot, p], device)

    swap = remote(img_ref, other, x_send.at[0], x_recv.at[0], partner)
    to_ahead = remote(txt_ref, txt_prev, x_send.at[1], x_recv.at[1], ahead)
    to_behind = remote(img_ref, img_next, x_send.at[2], x_recv.at[2], behind)
    give = remote(gi_other, gi_in, x_send.at[3], x_recv.at[3], partner)

    swap.start()

    @pl.when(has_right)
    def _():
        own_text(chip, right).start()

    @pl.when(has_left)
    def _():
        own_text(n, left).start()

    to_ahead.start()
    to_behind.start()

    def weights(dots, matching):
        logits = sharp * dots + bias
        if matching:
            hit = lax.broadcasted_iota(jnp.int32, dots.shape, 0) == lax.broadcasted_iota(
                jnp.int32, dots.shape, 1
            )
            sign = jnp.where(hit, 1.0, -1.0).astype(F32)
            return (-sign * (sharp / (1.0 + jnp.exp(sign * logits)))).astype(jnp.bfloat16)
        return (sharp / (1.0 + jnp.exp(-logits))).astype(jnp.bfloat16)

    def text_block(block_ref, b):
        for half, img, total in ((0, img_ref, gi_ref), (1, other, gi_other)):
            c = weights(contract(block_ref[...], img[...], 1, 1), False)
            coef[b, half] = c
            total[...] += contract(c, block_ref[...], 0, 0)

    def share(b, p):
        part = pl.ds(pl.multiple_of(p * piece, piece), piece)
        return contract(coef[b, 0, part, :], img_ref[...], 1, 0) + contract(
            coef[b, 1, part, :], other[...], 1, 0
        )

    c = weights(contract(txt_ref[...], img_ref[...], 1, 1), True)
    gi_ref[...] = contract(c, txt_ref[...], 0, 0)
    gt_ref[...] = contract(c, img_ref[...], 1, 0)
    swap.wait()
    c = weights(contract(txt_ref[...], other[...], 1, 1), False)
    gi_other[...] = contract(c, txt_ref[...], 0, 0)
    gt_ref[...] += contract(c, other[...], 1, 0)

    def send_on(b, slot, p, total, mean, device):
        middle = jnp.mean(total, axis=0, keepdims=True)
        gout[b, p] = (total - middle).astype(jnp.bfloat16)
        vout[b, p] = middle if mean is None else middle + mean
        sums(b, slot, p, device).start()
        means(b, slot, p, device).start()

    def arrived(slot, p):
        sums(0, slot, p, partner).wait_recv()
        means(0, slot, p, partner).wait_recv()

    def slot_right(b):
        return jnp.where(chip + 1 == b, n, b)

    def phase(t, carry):
        from_left, from_right = chip - t, chip + t
        for valid, b, more, device in (
            (from_left >= 0, from_left, has_right, right),
            (from_right < n, from_right, has_left, left),
        ):
            @pl.when(valid)
            def _():
                passed_text(b, partner).wait_recv()

                @pl.when(more)
                def _():
                    passed_text(b, device).start()

        for valid, b in ((from_left >= 0, from_left), (from_right < n, from_right)):
            @pl.when(valid)
            def _():
                text_block(tbuf.at[b], b)

        low, high = n - 1 - t, t

        @pl.when(jnp.logical_not(has_right))
        def _():
            @pl.loop(0, PIECES)
            def _(p):
                send_on(low, low, p, share(low, p), None, left)

        @pl.when(jnp.logical_not(has_left))
        def _():
            @pl.loop(0, PIECES)
            def _(p):
                send_on(high, slot_right(high), p, share(high, p), None, right)

        @pl.when(t == n - 1)
        def _():
            give.start()
            to_ahead.wait_recv()
            c = weights(contract(img_ref[...], txt_prev[...], 1, 1), False)
            gi_ref[...] += contract(c, txt_prev[...], 1, 0)
            to_behind.wait_recv()
            c = weights(contract(txt_ref[...], img_next[...], 1, 1), False)
            gt_ref[...] += contract(c, img_next[...], 1, 0)

        @pl.loop(0, PIECES)
        def _(p):
            @pl.when((low < chip) & has_right)
            def _():
                here = share(low, p)
                arrived(low, p)
                send_on(low, low, p, here + gin[low, p].astype(F32), vin[low, p], left)

            @pl.when((high > chip) & has_left)
            def _():
                here = share(high, p)
                arrived(high, p)
                send_on(
                    high, slot_right(high), p, here + gin[high, p].astype(F32), vin[high, p], right
                )

        for owner, slot in ((low == chip, chip), (high == chip, n)):
            @pl.when(owner)
            def _():
                @pl.loop(0, PIECES)
                def _(p):
                    arrived(slot, p)
                    part = pl.ds(pl.multiple_of(p * piece, piece), piece)
                    gt_ref[part, :] += gin[slot, p].astype(F32) + vin[slot, p]

        return carry

    lax.fori_loop(1, n, phase, 0)

    give.wait_recv()
    gi_ref[...] += gi_in[...]

    give.wait_send()
    to_ahead.wait_send()
    to_behind.wait_send()

    @pl.when(has_right)
    def _():
        own_text(chip, right).wait_send()

    @pl.when(has_left)
    def _():
        own_text(n, left).wait_send()

    @pl.loop(0, n)
    def _(b):
        @pl.when(((b < chip) & has_right) | ((b > chip) & has_left))
        def _():
            passed_text(b, partner).wait_send()

        @pl.when(b != chip)
        def _():
            @pl.loop(0, PIECES)
            def _(p):
                sums(b, b, p, partner).wait_send()
                means(b, b, p, partner).wait_send()


def solution(mesh):
    groups, members = mesh.shape["group"], mesh.shape["member"]
    n = members // 2

    def shards(images, texts, sharpness, offset):
        rows, width = images.shape
        piece = rows // PIECES
        bf16 = jnp.bfloat16
        out = jax.ShapeDtypeStruct((rows, width), F32)
        vmem = pl.BlockSpec(memory_space=pltpu.VMEM)
        smem = pl.BlockSpec(memory_space=pltpu.SMEM)
        dma = pltpu.SemaphoreType.DMA
        return pl.pallas_call(
            functools.partial(kernel, groups, n),
            out_shape=(out, out),
            in_specs=[smem, smem, vmem, vmem],
            out_specs=(vmem, vmem),
            scratch_shapes=[
                pltpu.VMEM((rows, width), bf16),
                pltpu.VMEM((rows, width), F32),
                pltpu.VMEM((rows, width), F32),
                pltpu.VMEM((rows, width), bf16),
                pltpu.VMEM((rows, width), bf16),
                pltpu.VMEM((n, rows, width), bf16),
                pltpu.VMEM((n, 2, rows, rows), bf16),
                pltpu.VMEM((n + 1, PIECES, piece, width), bf16),
                pltpu.VMEM((n, PIECES, piece, width), bf16),
                pltpu.VMEM((n + 1, PIECES, 1, width), F32),
                pltpu.VMEM((n, PIECES, 1, width), F32),
                dma((n + 1,)),
                dma((n,)),
                dma((n, PIECES)),
                dma((n + 1, PIECES)),
                dma((n, PIECES)),
                dma((n + 1, PIECES)),
                dma((4,)),
                dma((4,)),
            ],
            compiler_params=pltpu.CompilerParams(
                collective_id=0, has_side_effects=True, vmem_limit_bytes=60 * 1024 * 1024
            ),
        )(sharpness, offset, images, texts)

    spec = P(("group", "member"), None)
    return jax.shard_map(
        shards, mesh=mesh, in_specs=(spec, spec, P(), P()), out_specs=(spec, spec), check_vma=False
    )
```

```python
import functools

import jax
import jax.numpy as jnp
from jax import lax
from jax.experimental import pallas as pl
from jax.experimental.pallas import tpu as pltpu
from jax.sharding import PartitionSpec as P

MESH = pl.DeviceIdType.MESH
F32 = jnp.float32
PIECES = 4
SKEW = 2


def contract(a, b, da, db):
    return lax.dot_general(a, b, (((da,), (db,)), ((), ())), preferred_element_type=F32)


def kernel(
    groups, n, sharp_ref, bias_ref, img_ref, txt_ref, gi_ref, gt_ref,
    other, gi_other, gi_in, txt_prev, img_next, tbuf, coef, gin, gout, vin, vout,
    t_send, t_recv, g_send, g_recv, v_send, v_recv, x_send, x_recv,
):
    rows, width = img_ref.shape
    piece = rows // PIECES
    group = lax.axis_index("group")
    member = lax.axis_index("member")
    chip, core = member // 2, member % 2
    partner = (group, member + 1 - 2 * core)
    ahead = ((group + 1) % groups, member)
    behind = ((group + groups - 1) % groups, member)
    right, left = (group, member + 2), (group, member - 2)
    has_right, has_left = chip + 1 < n, chip > 0
    sharp, bias = sharp_ref[0], bias_ref[0]

    barrier = pltpu.get_barrier_semaphore()
    for device in (partner, ahead, behind):
        pl.semaphore_signal(barrier, inc=1, device_id=device, device_id_type=MESH)
    for exists, device in ((has_right, right), (has_left, left)):
        @pl.when(exists)
        def _():
            pl.semaphore_signal(barrier, inc=1, device_id=device, device_id_type=MESH)
    pl.semaphore_wait(barrier, 3 + has_right.astype(jnp.int32) + has_left.astype(jnp.int32))

    def remote(src, dst, send, recv, device):
        return pltpu.make_async_remote_copy(
            src_ref=src, dst_ref=dst, send_sem=send, recv_sem=recv,
            device_id=device, device_id_type=MESH,
        )

    def part_of(p):
        return pl.ds(pl.multiple_of(p * piece, piece), piece)

    def own_text(slot, p, device):
        return remote(
            txt_ref.at[part_of(p)], tbuf.at[chip, part_of(p)],
            t_send.at[slot, p], t_recv.at[chip, p], device,
        )

    def passed_text(b, p, device):
        block = tbuf.at[b, part_of(p)]
        return remote(block, block, t_send.at[b, p], t_recv.at[b, p], device)

    def sums(b, slot, p, device):
        return remote(gout.at[b, p], gin.at[slot, p], g_send.at[b, p], g_recv.at[slot, p], device)

    def means(b, slot, p, device):
        return remote(vout.at[b, p], vin.at[slot, p], v_send.at[b, p], v_recv.at[slot, p], device)

    swap = remote(img_ref, other, x_send.at[0], x_recv.at[0], partner)
    to_ahead = remote(txt_ref, txt_prev, x_send.at[1], x_recv.at[1], ahead)
    to_behind = remote(img_ref, img_next, x_send.at[2], x_recv.at[2], behind)
    give = remote(gi_other, gi_in, x_send.at[3], x_recv.at[3], partner)

    swap.start()

    for p in range(PIECES):
        @pl.when(has_right)
        def _():
            own_text(chip, p, right).start()

        @pl.when(has_left)
        def _():
            own_text(n, p, left).start()

    to_ahead.start()
    to_behind.start()

    def weights(dots, matching):
        logits = sharp * dots + bias
        if matching:
            hit = lax.broadcasted_iota(jnp.int32, dots.shape, 0) == lax.broadcasted_iota(
                jnp.int32, dots.shape, 1
            )
            sign = jnp.where(hit, 1.0, -1.0).astype(F32)
            return (-sign * (sharp / (1.0 + jnp.exp(sign * logits)))).astype(jnp.bfloat16)
        return (sharp / (1.0 + jnp.exp(-logits))).astype(jnp.bfloat16)

    def weigh(b, part):
        for half, img in ((0, img_ref), (1, other)):
            coef[b, half, part, :] = weights(contract(tbuf[b, part, :], img[...], 1, 1), False)

    def add_images(b):
        for half, total in ((0, gi_ref), (1, gi_other)):
            total[...] += contract(coef[b, half], tbuf[b], 0, 0)

    def share(b, p):
        part = part_of(p)
        return contract(coef[b, 0, part, :], img_ref[...], 1, 0) + contract(
            coef[b, 1, part, :], other[...], 1, 0
        )

    c = weights(contract(txt_ref[...], img_ref[...], 1, 1), True)
    gi_ref[...] = contract(c, txt_ref[...], 0, 0)
    gt_ref[...] = contract(c, img_ref[...], 1, 0)
    swap.wait()
    c = weights(contract(txt_ref[...], other[...], 1, 1), False)
    gi_other[...] = contract(c, txt_ref[...], 0, 0)
    gt_ref[...] += contract(c, other[...], 1, 0)

    def send_on(b, slot, p, total, mean, device):
        middle = jnp.mean(total, axis=0, keepdims=True)
        gout[b, p] = (total - middle).astype(jnp.bfloat16)
        vout[b, p] = middle if mean is None else middle + mean
        sums(b, slot, p, device).start()
        means(b, slot, p, device).start()

    def arrived(slot, p):
        sums(0, slot, p, partner).wait_recv()
        means(0, slot, p, partner).wait_recv()

    def slot_right(b):
        return jnp.where(chip + 1 == b, n, b)

    def collect(low, high):
        for owner, slot in ((low == chip, chip), (high == chip, n)):
            @pl.when(owner)
            def _():
                @pl.loop(0, PIECES)
                def _(p):
                    arrived(slot, p)
                    gt_ref[part_of(p), :] += gin[slot, p].astype(F32) + vin[slot, p]

    def phase(t, carry):
        from_left, from_right = chip - t, chip + t
        low, high = n - 1 - t, t
        sides = (
            (from_left >= 0, from_left, has_right, right, left, from_left),
            (from_right < n, from_right, has_left, left, right, slot_right(from_right)),
        )

        @pl.loop(0, PIECES)
        def _(p):
            for valid, b, more, onward, back, slot in sides:
                @pl.when(valid)
                def _():
                    passed_text(b, p, partner).wait_recv()

                    @pl.when(more)
                    def _():
                        passed_text(b, p, onward).start()

                    @pl.when(jnp.logical_not(more))
                    def _():
                        weigh(b, part_of(p))
                        send_on(b, slot, p, share(b, p), None, back)

        for valid, b, more, onward, back, slot in sides:
            @pl.when(valid)
            def _():
                @pl.when(more)
                def _():
                    weigh(b, pl.ds(0, rows))

                add_images(b)

        @pl.when(t >= 2)
        def _():
            collect(low + 1, high - 1)

        @pl.when(t == n - 1)
        def _():
            give.start()
            to_ahead.wait_recv()
            c = weights(contract(img_ref[...], txt_prev[...], 1, 1), False)
            gi_ref[...] += contract(c, txt_prev[...], 1, 0)
            to_behind.wait_recv()
            c = weights(contract(txt_ref[...], img_next[...], 1, 1), False)
            gt_ref[...] += contract(c, img_next[...], 1, 0)

        @pl.when(has_left & has_right & ((low < chip) | (high > chip)))
        def _():
            @pl.loop(0, PIECES + SKEW * (n - 1))
            def _(step):
                p_low, p_high = step - SKEW * (n - 1 - chip), step - SKEW * chip

                @pl.when((low < chip) & (p_low >= 0) & (p_low < PIECES))
                def _():
                    here = share(low, p_low)
                    arrived(low, p_low)
                    total = here + gin[low, p_low].astype(F32)
                    send_on(low, low, p_low, total, vin[low, p_low], left)

                @pl.when((high > chip) & (p_high >= 0) & (p_high < PIECES))
                def _():
                    here = share(high, p_high)
                    arrived(high, p_high)
                    total = here + gin[high, p_high].astype(F32)
                    send_on(high, slot_right(high), p_high, total, vin[high, p_high], right)

        return carry

    lax.fori_loop(1, n, phase, 0)
    collect(0, n - 1)

    give.wait_recv()
    gi_ref[...] += gi_in[...]

    give.wait_send()
    to_ahead.wait_send()
    to_behind.wait_send()

    @pl.loop(0, PIECES)
    def _(p):
        @pl.when(has_right)
        def _():
            own_text(chip, p, right).wait_send()

        @pl.when(has_left)
        def _():
            own_text(n, p, left).wait_send()

        @pl.loop(0, n)
        def _(b):
            @pl.when(((b < chip) & has_right) | ((b > chip) & has_left))
            def _():
                passed_text(b, p, partner).wait_send()

            @pl.when(b != chip)
            def _():
                sums(b, b, p, partner).wait_send()
                means(b, b, p, partner).wait_send()


def solution(mesh):
    groups, members = mesh.shape["group"], mesh.shape["member"]
    n = members // 2

    def shards(images, texts, sharpness, offset):
        rows, width = images.shape
        piece = rows // PIECES
        bf16 = jnp.bfloat16
        out = jax.ShapeDtypeStruct((rows, width), F32)
        vmem = pl.BlockSpec(memory_space=pltpu.VMEM)
        smem = pl.BlockSpec(memory_space=pltpu.SMEM)
        dma = pltpu.SemaphoreType.DMA
        return pl.pallas_call(
            functools.partial(kernel, groups, n),
            out_shape=(out, out),
            in_specs=[smem, smem, vmem, vmem],
            out_specs=(vmem, vmem),
            scratch_shapes=[
                pltpu.VMEM((rows, width), bf16),
                pltpu.VMEM((rows, width), F32),
                pltpu.VMEM((rows, width), F32),
                pltpu.VMEM((rows, width), bf16),
                pltpu.VMEM((rows, width), bf16),
                pltpu.VMEM((n, rows, width), bf16),
                pltpu.VMEM((n, 2, rows, rows), bf16),
                pltpu.VMEM((n + 1, PIECES, piece, width), bf16),
                pltpu.VMEM((n, PIECES, piece, width), bf16),
                pltpu.VMEM((n + 1, PIECES, 1, width), F32),
                pltpu.VMEM((n, PIECES, 1, width), F32),
                dma((n + 1, PIECES)),
                dma((n, PIECES)),
                dma((n, PIECES)),
                dma((n + 1, PIECES)),
                dma((n, PIECES)),
                dma((n + 1, PIECES)),
                dma((4,)),
                dma((4,)),
            ],
            compiler_params=pltpu.CompilerParams(
                collective_id=0, has_side_effects=True, vmem_limit_bytes=60 * 1024 * 1024
            ),
        )(sharpness, offset, images, texts)

    spec = P(("group", "member"), None)
    return jax.shard_map(
        shards, mesh=mesh, in_specs=(spec, spec, P(), P()), out_specs=(spec, spec), check_vma=False
    )
```

```python
import functools

import jax
import jax.numpy as jnp
from jax import lax
from jax.experimental import pallas as pl
from jax.experimental.pallas import tpu as pltpu
from jax.sharding import PartitionSpec as P

MESH = pl.DeviceIdType.MESH
F32 = jnp.float32
PIECES = 4
SKEW = 2
EARLY = 2


def contract(a, b, da, db):
    return lax.dot_general(a, b, (((da,), (db,)), ((), ())), preferred_element_type=F32)


def kernel(
    groups, n, sharp_ref, bias_ref, img_ref, txt_ref, gi_ref, gt_ref,
    other, gi_other, gi_in, txt_prev, img_next, tbuf, coef, gin, gout, vin, vout,
    t_send, t_recv, g_send, g_recv, v_send, v_recv, x_send, x_recv,
):
    rows, width = img_ref.shape
    piece = rows // PIECES
    group = lax.axis_index("group")
    member = lax.axis_index("member")
    chip, core = member // 2, member % 2
    partner = (group, member + 1 - 2 * core)
    ahead = ((group + 1) % groups, member)
    behind = ((group + groups - 1) % groups, member)
    right, left = (group, member + 2), (group, member - 2)
    has_right, has_left = chip + 1 < n, chip > 0
    sharp, bias = sharp_ref[0], bias_ref[0]

    barrier = pltpu.get_barrier_semaphore()
    for device in (partner, ahead, behind):
        pl.semaphore_signal(barrier, inc=1, device_id=device, device_id_type=MESH)
    for exists, device in ((has_right, right), (has_left, left)):
        @pl.when(exists)
        def _():
            pl.semaphore_signal(barrier, inc=1, device_id=device, device_id_type=MESH)
    pl.semaphore_wait(barrier, 3 + has_right.astype(jnp.int32) + has_left.astype(jnp.int32))

    def remote(src, dst, send, recv, device):
        return pltpu.make_async_remote_copy(
            src_ref=src, dst_ref=dst, send_sem=send, recv_sem=recv,
            device_id=device, device_id_type=MESH,
        )

    def part_of(p):
        return pl.ds(pl.multiple_of(p * piece, piece), piece)

    def own_text(slot, p, device):
        return remote(
            txt_ref.at[part_of(p)], tbuf.at[chip, part_of(p)],
            t_send.at[slot, p], t_recv.at[chip, p], device,
        )

    def passed_text(b, p, device):
        block = tbuf.at[b, part_of(p)]
        return remote(block, block, t_send.at[b, p], t_recv.at[b, p], device)

    def sums(b, slot, p, device):
        return remote(gout.at[b, p], gin.at[slot, p], g_send.at[b, p], g_recv.at[slot, p], device)

    def means(b, slot, p, device):
        return remote(vout.at[b, p], vin.at[slot, p], v_send.at[b, p], v_recv.at[slot, p], device)

    swap = remote(img_ref, other, x_send.at[0], x_recv.at[0], partner)
    to_ahead = remote(txt_ref, txt_prev, x_send.at[1], x_recv.at[1], ahead)
    to_behind = remote(img_ref, img_next, x_send.at[2], x_recv.at[2], behind)
    give = remote(gi_other, gi_in, x_send.at[3], x_recv.at[3], partner)

    swap.start()

    for p in range(PIECES):
        @pl.when(has_right)
        def _():
            own_text(chip, p, right).start()

        @pl.when(has_left)
        def _():
            own_text(n, p, left).start()

    to_ahead.start()
    to_behind.start()

    def weights(dots, matching):
        logits = sharp * dots + bias
        if matching:
            hit = lax.broadcasted_iota(jnp.int32, dots.shape, 0) == lax.broadcasted_iota(
                jnp.int32, dots.shape, 1
            )
            sign = jnp.where(hit, 1.0, -1.0).astype(F32)
            return (-sign * (sharp / (1.0 + jnp.exp(sign * logits)))).astype(jnp.bfloat16)
        return (sharp / (1.0 + jnp.exp(-logits))).astype(jnp.bfloat16)

    def weigh(b, part):
        for half, img in ((0, img_ref), (1, other)):
            coef[b, half, part, :] = weights(contract(tbuf[b, part, :], img[...], 1, 1), False)

    def add_images(b):
        for half, total in ((0, gi_ref), (1, gi_other)):
            total[...] += contract(coef[b, half], tbuf[b], 0, 0)

    def share(b, p):
        part = part_of(p)
        return contract(coef[b, 0, part, :], img_ref[...], 1, 0) + contract(
            coef[b, 1, part, :], other[...], 1, 0
        )

    c = weights(contract(txt_ref[...], img_ref[...], 1, 1), True)
    gi_ref[...] = contract(c, txt_ref[...], 0, 0)
    gt_ref[...] = contract(c, img_ref[...], 1, 0)
    swap.wait()
    c = weights(contract(txt_ref[...], other[...], 1, 1), False)
    gi_other[...] = contract(c, txt_ref[...], 0, 0)
    gt_ref[...] += contract(c, other[...], 1, 0)

    def send_on(b, slot, p, total, mean, device):
        middle = jnp.mean(total, axis=0, keepdims=True)
        gout[b, p] = (total - middle).astype(jnp.bfloat16)
        vout[b, p] = middle if mean is None else middle + mean
        sums(b, slot, p, device).start()
        means(b, slot, p, device).start()

    def arrived(slot, p):
        sums(0, slot, p, partner).wait_recv()
        means(0, slot, p, partner).wait_recv()

    def slot_right(b):
        return jnp.where(chip + 1 == b, n, b)

    def phase(t, carry):
        from_left, from_right = chip - t, chip + t
        low, high = n - 1 - t, t
        sides = (
            (from_left >= 0, from_left, has_right, right, left, from_left),
            (from_right < n, from_right, has_left, left, right, slot_right(from_right)),
        )

        @pl.loop(0, PIECES)
        def _(p):
            for valid, b, more, onward, back, slot in sides:
                @pl.when(valid)
                def _():
                    passed_text(b, p, partner).wait_recv()

                    @pl.when(more)
                    def _():
                        passed_text(b, p, onward).start()

                    @pl.when(jnp.logical_not(more))
                    def _():
                        weigh(b, part_of(p))

                        @pl.when((t > 1) | (p < EARLY))
                        def _():
                            send_on(b, slot, p, share(b, p), None, back)

        for more, b, slot, back in (
            (has_right, chip - 1, chip - 1, left),
            (has_left, chip + 1, n, right),
        ):
            @pl.when((t == n - 1) & jnp.logical_not(more))
            def _():
                @pl.loop(EARLY, PIECES)
                def _(p):
                    send_on(b, slot, p, share(b, p), None, back)

        for valid, b, more, onward, back, slot in sides:
            @pl.when(valid)
            def _():
                @pl.when(more)
                def _():
                    weigh(b, pl.ds(0, rows))

                add_images(b)

        @pl.when(t == n - 1)
        def _():
            give.start()

        @pl.when(has_left & has_right & ((low < chip) | (high > chip)))
        def _():
            @pl.loop(0, PIECES + SKEW * (n - 1))
            def _(step):
                p_low, p_high = step - SKEW * (n - 1 - chip), step - SKEW * chip

                @pl.when((low < chip) & (p_low >= 0) & (p_low < PIECES))
                def _():
                    here = share(low, p_low)
                    arrived(low, p_low)
                    total = here + gin[low, p_low].astype(F32)
                    send_on(low, low, p_low, total, vin[low, p_low], left)

                @pl.when((high > chip) & (p_high >= 0) & (p_high < PIECES))
                def _():
                    here = share(high, p_high)
                    arrived(high, p_high)
                    total = here + gin[high, p_high].astype(F32)
                    send_on(high, slot_right(high), p_high, total, vin[high, p_high], right)

        return carry

    lax.fori_loop(1, n, phase, 0)

    to_ahead.wait_recv()
    c = weights(contract(img_ref[...], txt_prev[...], 1, 1), False)
    gi_ref[...] += contract(c, txt_prev[...], 1, 0)
    to_behind.wait_recv()
    c = weights(contract(txt_ref[...], img_next[...], 1, 1), False)
    gt_ref[...] += contract(c, img_next[...], 1, 0)
    give.wait_recv()
    gi_ref[...] += gi_in[...]

    for exists, slot in ((has_left, n), (has_right, chip)):
        @pl.when(exists)
        def _():
            @pl.loop(0, PIECES)
            def _(p):
                arrived(slot, p)
                gt_ref[part_of(p), :] += gin[slot, p].astype(F32) + vin[slot, p]

    give.wait_send()
    to_ahead.wait_send()
    to_behind.wait_send()

    @pl.loop(0, PIECES)
    def _(p):
        @pl.when(has_right)
        def _():
            own_text(chip, p, right).wait_send()

        @pl.when(has_left)
        def _():
            own_text(n, p, left).wait_send()

        @pl.loop(0, n)
        def _(b):
            @pl.when(((b < chip) & has_right) | ((b > chip) & has_left))
            def _():
                passed_text(b, p, partner).wait_send()

            @pl.when(b != chip)
            def _():
                sums(b, b, p, partner).wait_send()
                means(b, b, p, partner).wait_send()


def solution(mesh):
    groups, members = mesh.shape["group"], mesh.shape["member"]
    n = members // 2

    def shards(images, texts, sharpness, offset):
        rows, width = images.shape
        piece = rows // PIECES
        bf16 = jnp.bfloat16
        out = jax.ShapeDtypeStruct((rows, width), F32)
        vmem = pl.BlockSpec(memory_space=pltpu.VMEM)
        smem = pl.BlockSpec(memory_space=pltpu.SMEM)
        dma = pltpu.SemaphoreType.DMA
        return pl.pallas_call(
            functools.partial(kernel, groups, n),
            out_shape=(out, out),
            in_specs=[smem, smem, vmem, vmem],
            out_specs=(vmem, vmem),
            scratch_shapes=[
                pltpu.VMEM((rows, width), bf16),
                pltpu.VMEM((rows, width), F32),
                pltpu.VMEM((rows, width), F32),
                pltpu.VMEM((rows, width), bf16),
                pltpu.VMEM((rows, width), bf16),
                pltpu.VMEM((n, rows, width), bf16),
                pltpu.VMEM((n, 2, rows, rows), bf16),
                pltpu.VMEM((n + 1, PIECES, piece, width), bf16),
                pltpu.VMEM((n, PIECES, piece, width), bf16),
                pltpu.VMEM((n + 1, PIECES, 1, width), F32),
                pltpu.VMEM((n, PIECES, 1, width), F32),
                dma((n + 1, PIECES)),
                dma((n, PIECES)),
                dma((n, PIECES)),
                dma((n + 1, PIECES)),
                dma((n, PIECES)),
                dma((n + 1, PIECES)),
                dma((4,)),
                dma((4,)),
            ],
            compiler_params=pltpu.CompilerParams(
                collective_id=0, has_side_effects=True, vmem_limit_bytes=60 * 1024 * 1024
            ),
        )(sharpness, offset, images, texts)

    spec = P(("group", "member"), None)
    return jax.shard_map(
        shards, mesh=mesh, in_specs=(spec, spec, P(), P()), out_specs=(spec, spec), check_vma=False
    )
```

```python
import functools

import jax
import jax.numpy as jnp
from jax import lax
from jax.experimental import pallas as pl
from jax.experimental.pallas import tpu as pltpu
from jax.sharding import PartitionSpec as P

MESH = pl.DeviceIdType.MESH
F32 = jnp.float32
PIECES = 4
SKEW = 2
EARLY = 2


def contract(a, b, da, db):
    return lax.dot_general(a, b, (((da,), (db,)), ((), ())), preferred_element_type=F32)


def kernel(
    groups, n, sharp_ref, bias_ref, img_ref, txt_ref, gi_ref, gt_ref,
    other, gi_other, gi_in, txt_prev, img_next, tbuf, coef, gin, gout, vin, vout,
    t_send, t_recv, g_send, g_recv, v_send, v_recv, x_send, x_recv,
):
    rows, width = img_ref.shape
    piece = rows // PIECES
    group = lax.axis_index("group")
    member = lax.axis_index("member")
    chip, core = member // 2, member % 2
    partner = (group, member + 1 - 2 * core)
    ahead = ((group + 1) % groups, member)
    behind = ((group + groups - 1) % groups, member)
    right, left = (group, member + 2), (group, member - 2)
    has_right, has_left = chip + 1 < n, chip > 0
    sharp, bias = sharp_ref[0], bias_ref[0]

    barrier = pltpu.get_barrier_semaphore()
    for device in (partner, ahead, behind):
        pl.semaphore_signal(barrier, inc=1, device_id=device, device_id_type=MESH)
    for exists, device in ((has_right, right), (has_left, left)):
        @pl.when(exists)
        def _():
            pl.semaphore_signal(barrier, inc=1, device_id=device, device_id_type=MESH)
    pl.semaphore_wait(barrier, 3 + has_right.astype(jnp.int32) + has_left.astype(jnp.int32))

    def remote(src, dst, send, recv, device):
        return pltpu.make_async_remote_copy(
            src_ref=src, dst_ref=dst, send_sem=send, recv_sem=recv,
            device_id=device, device_id_type=MESH,
        )

    def part_of(p):
        return pl.ds(pl.multiple_of(p * piece, piece), piece)

    def own_text(slot, p, device):
        return remote(
            txt_ref.at[part_of(p)], tbuf.at[chip, part_of(p)],
            t_send.at[slot, p], t_recv.at[chip, p], device,
        )

    def passed_text(b, p, device):
        block = tbuf.at[b, part_of(p)]
        return remote(block, block, t_send.at[b, p], t_recv.at[b, p], device)

    def sums(b, slot, p, device):
        return remote(gout.at[b, p], gin.at[slot, p], g_send.at[b, p], g_recv.at[slot, p], device)

    def means(b, slot, p, device):
        return remote(vout.at[b, p], vin.at[slot, p], v_send.at[b, p], v_recv.at[slot, p], device)

    swap = remote(img_ref, other, x_send.at[0], x_recv.at[0], partner)
    to_ahead = remote(txt_ref, txt_prev, x_send.at[1], x_recv.at[1], ahead)
    to_behind = remote(img_ref, img_next, x_send.at[2], x_recv.at[2], behind)
    give = remote(gi_other, gi_in, x_send.at[3], x_recv.at[3], partner)

    swap.start()

    for p in range(PIECES):
        @pl.when(has_right)
        def _():
            own_text(chip, p, right).start()

        @pl.when(has_left)
        def _():
            own_text(n, p, left).start()

    to_ahead.start()
    to_behind.start()

    def weights(dots, matching):
        logits = sharp * dots + bias
        if matching:
            hit = lax.broadcasted_iota(jnp.int32, dots.shape, 0) == lax.broadcasted_iota(
                jnp.int32, dots.shape, 1
            )
            sign = jnp.where(hit, 1.0, -1.0).astype(F32)
            return (-sign * (sharp / (1.0 + jnp.exp(sign * logits)))).astype(jnp.bfloat16)
        return (sharp / (1.0 + jnp.exp(-logits))).astype(jnp.bfloat16)

    def weigh(b, part):
        for half, img in ((0, img_ref), (1, other)):
            coef[b, half, part, :] = weights(contract(tbuf[b, part, :], img[...], 1, 1), False)

    def add_images(b):
        for half, total in ((0, gi_ref), (1, gi_other)):
            total[...] += contract(coef[b, half], tbuf[b], 0, 0)

    def share(b, p):
        part = part_of(p)
        return contract(coef[b, 0, part, :], img_ref[...], 1, 0) + contract(
            coef[b, 1, part, :], other[...], 1, 0
        )

    c = weights(contract(txt_ref[...], img_ref[...], 1, 1), True)
    gi_ref[...] = contract(c, txt_ref[...], 0, 0)
    gt_ref[...] = contract(c, img_ref[...], 1, 0)
    swap.wait()
    c = weights(contract(txt_ref[...], other[...], 1, 1), False)
    gi_other[...] = contract(c, txt_ref[...], 0, 0)
    gt_ref[...] += contract(c, other[...], 1, 0)

    def send_on(b, slot, p, total, mean, device):
        middle = jnp.mean(total, axis=0, keepdims=True)
        gout[b, p] = (total - middle).astype(jnp.bfloat16)
        vout[b, p] = middle if mean is None else middle + mean
        sums(b, slot, p, device).start()
        means(b, slot, p, device).start()

    def arrived(slot, p):
        sums(0, slot, p, partner).wait_recv()
        means(0, slot, p, partner).wait_recv()

    def slot_right(b):
        return jnp.where(chip + 1 == b, n, b)

    def phase(t, carry):
        from_left, from_right = chip - t, chip + t
        low, high = n - 1 - t, t
        sides = (
            (from_left >= 0, from_left, has_right, right, left, from_left),
            (from_right < n, from_right, has_left, left, right, slot_right(from_right)),
        )

        @pl.loop(0, PIECES)
        def _(p):
            for valid, b, more, onward, back, slot in sides:
                @pl.when(valid)
                def _():
                    passed_text(b, p, partner).wait_recv()

                    @pl.when(more)
                    def _():
                        passed_text(b, p, onward).start()

                    @pl.when(jnp.logical_not(more))
                    def _():
                        weigh(b, part_of(p))

                        @pl.when((t > 1) | (p < EARLY))
                        def _():
                            send_on(b, slot, p, share(b, p), None, back)

        for more, b, slot, back in (
            (has_right, chip - 1, chip - 1, left),
            (has_left, chip + 1, n, right),
        ):
            @pl.when((t == n - 1) & jnp.logical_not(more))
            def _():
                @pl.loop(EARLY, PIECES)
                def _(p):
                    send_on(b, slot, p, share(b, p), None, back)

        for valid, b, more, onward, back, slot in sides:
            @pl.when(valid)
            def _():
                @pl.when(more)
                def _():
                    weigh(b, pl.ds(0, rows))

                add_images(b)

        @pl.when(t == n - 1)
        def _():
            give.start()

        @pl.when(has_left & has_right & ((low < chip) | (high > chip)))
        def _():
            @pl.loop(0, PIECES + SKEW * (n - 1))
            def _(step):
                p_low, p_high = step - SKEW * (n - 1 - chip), step - SKEW * chip

                @pl.when((low < chip) & (p_low >= 0) & (p_low < PIECES))
                def _():
                    here = share(low, p_low)
                    arrived(low, p_low)
                    total = here + gin[low, p_low].astype(F32)
                    send_on(low, low, p_low, total, vin[low, p_low], left)

                @pl.when((high > chip) & (p_high >= 0) & (p_high < PIECES))
                def _():
                    here = share(high, p_high)
                    arrived(high, p_high)
                    total = here + gin[high, p_high].astype(F32)
                    send_on(high, slot_right(high), p_high, total, vin[high, p_high], right)

        return carry

    lax.fori_loop(1, n, phase, 0)

    to_ahead.wait_recv()
    c = weights(contract(img_ref[...], txt_prev[...], 1, 1), False)
    gi_ref[...] += contract(c, txt_prev[...], 1, 0)
    to_behind.wait_recv()
    c = weights(contract(txt_ref[...], img_next[...], 1, 1), False)
    gt_ref[...] += contract(c, img_next[...], 1, 0)
    give.wait_recv()
    gi_ref[...] += gi_in[...]

    for exists, slot in ((has_left, n), (has_right, chip)):
        @pl.when(exists)
        def _():
            @pl.loop(0, PIECES)
            def _(p):
                arrived(slot, p)
                gt_ref[part_of(p), :] += gin[slot, p].astype(F32) + vin[slot, p]

    give.wait_send()
    to_ahead.wait_send()
    to_behind.wait_send()

    @pl.loop(0, PIECES)
    def _(p):
        @pl.when(has_right)
        def _():
            own_text(chip, p, right).wait_send()

        @pl.when(has_left)
        def _():
            own_text(n, p, left).wait_send()

        @pl.loop(0, n)
        def _(b):
            @pl.when(((b < chip) & has_right) | ((b > chip) & has_left))
            def _():
                passed_text(b, p, partner).wait_send()

            @pl.when(b != chip)
            def _():
                sums(b, b, p, partner).wait_send()
                means(b, b, p, partner).wait_send()


def solution(mesh):
    groups, members = mesh.shape["group"], mesh.shape["member"]
    n = members // 2

    def shards(images, texts, sharpness, offset):
        rows, width = images.shape
        piece = rows // PIECES
        bf16 = jnp.bfloat16
        out = jax.ShapeDtypeStruct((rows, width), F32)
        vmem = pl.BlockSpec(memory_space=pltpu.VMEM)
        smem = pl.BlockSpec(memory_space=pltpu.SMEM)
        dma = pltpu.SemaphoreType.DMA
        return pl.pallas_call(
            functools.partial(kernel, groups, n),
            out_shape=(out, out),
            in_specs=[smem, smem, vmem, vmem],
            out_specs=(vmem, vmem),
            scratch_shapes=[
                pltpu.VMEM((rows, width), bf16),
                pltpu.VMEM((rows, width), F32),
                pltpu.VMEM((rows, width), F32),
                pltpu.VMEM((rows, width), bf16),
                pltpu.VMEM((rows, width), bf16),
                pltpu.VMEM((n, rows, width), bf16),
                pltpu.VMEM((n, 2, rows, rows), bf16),
                pltpu.VMEM((n + 1, PIECES, piece, width), bf16),
                pltpu.VMEM((n, PIECES, piece, width), bf16),
                pltpu.VMEM((n + 1, PIECES, 1, width), F32),
                pltpu.VMEM((n, PIECES, 1, width), F32),
                dma((n + 1, PIECES)),
                dma((n, PIECES)),
                dma((n, PIECES)),
                dma((n + 1, PIECES)),
                dma((n, PIECES)),
                dma((n + 1, PIECES)),
                dma((4,)),
                dma((4,)),
            ],
            compiler_params=pltpu.CompilerParams(
                collective_id=0, has_side_effects=True, vmem_limit_bytes=min(60, 16 + 3 * n) * 1024 * 1024
            ),
        )(sharpness, offset, images, texts)

    spec = P(("group", "member"), None)
    return jax.shard_map(
        shards, mesh=mesh, in_specs=(spec, spec, P(), P()), out_specs=(spec, spec), check_vma=False
    )
```
